32 devices in a mesh: row: 16 (over z, y, core), col: 2 (over x).
Axes of the slice: x: 2, y: 2, z: 4, core: 2. Of those that a mesh axis runs over, the one named last changes fastest.
Arguments:
- slab: bfloat16 [4096, 4096], P('row', 'col'), may hold values from -6 to 6
- slab_mask: int32 [32, 32], P('row', 'col'), may hold values 0 or 1
- density: bfloat16 [4096, 4096], P('row', 'col'), may hold values from -0.125 to 0.125
- block_mask: int32 [32, 32], P('row', 'col'), may hold values 0 or 1
Outputs:
- purified: bfloat16 [4096, 4096], P('row', 'col')
The draws below stay inside these ranges and needn't reach their ends.
Inputs may be any that keep to these rules, and one draw needn't show every extreme that they name: `slab_mask`: 0 or 1 per block. `block_mask`: 0 or 1 per block.
All inputs are finite; a program needn't handle non-finite values.
Results may differ from the reference program's by a relative error of at most 0.005.
Values may be sent and summed in bfloat16 or wider, within the bound.
A program may use at most 64 MiB of HBM per device.

```python
import jax
import jax.numpy as jnp

BLOCK = 128
M = 4096
R = 4096


def plant(drawn, stream_key, least, largest):
    index_at = [jax.random.randint(jax.random.fold_in(stream_key, axis), (), 0, length) for axis, length in enumerate(drawn.shape)]
    widest = drawn.shape.index(max(drawn.shape))
    beside = index_at[:widest] + [(index_at[widest] + 1) % drawn.shape[widest]] + index_at[widest + 1:]
    return drawn.at[tuple(index_at)].set(least).at[tuple(beside)].set(largest)


def steps_of(key, dims, cuts, least, high):
    def one(position, shards_of):
        heights = jax.random.uniform(jax.random.fold_in(jax.random.fold_in(key, 6), position), (shards_of,), jnp.float32, least / len(cuts), high / len(cuts))
        return jnp.repeat(jnp.exp(heights), dims[position] // shards_of).reshape((-1,) + (1,) * (len(dims) - position - 1))

    loudness = one(*cuts[0])
    for cut in cuts[1:]:
        loudness = loudness * one(*cut)
    return loudness


def gaussian(stream_key, shape, scale, bound, cuts=(), dtype=jnp.bfloat16):
    result = jax.random.normal(stream_key, shape, jnp.float32) * scale
    if len(cuts) > 0:
        result = steps_of(stream_key, shape, cuts, -0.22, 0.18) * result
    return jnp.clip(result, min=-bound, max=bound).astype(dtype)


def setup_inputs(seed: int = 0) -> dict:
    key_list = jax.random.split(jax.random.key(seed), 5)
    slab = gaussian(key_list[0], (R, M), 1.0, 6.0, ((0, 16), (1, 2)))
    slab_mask = plant((jax.random.randint(key_list[1], (R // BLOCK, M // BLOCK), 0, 2) < 1).astype(jnp.int32), jax.random.fold_in(key_list[1], 1), 0, 1)
    density = gaussian(key_list[2], (M, M), (M // 2) ** -0.5, 0.125, ((0, 16), (1, 2)))
    block_mask = plant((jax.random.randint(key_list[3], (M // BLOCK, M // BLOCK), 0, 2) < 1).astype(jnp.int32), jax.random.fold_in(key_list[3], 1), 0, 1)
    return dict(slab=slab, slab_mask=slab_mask, density=density, block_mask=block_mask)


def expand(mask):
    return jnp.repeat(jnp.repeat(mask, BLOCK, axis=0), BLOCK, axis=1)


def reference(slab, slab_mask, density, block_mask):
    dense = density * expand(block_mask).astype(jnp.bfloat16)
    rows = slab * expand(slab_mask).astype(jnp.bfloat16)
    square = jnp.dot(rows, dense, preferred_element_type=jnp.float32).astype(jnp.bfloat16)
    cube = jnp.dot(square, dense, preferred_element_type=jnp.float32)
    return (3.0 * square.astype(jnp.float32) - 2.0 * cube).astype(jnp.bfloat16)
```

```python
import functools

import jax
import jax.numpy as jnp
from jax import lax
from jax.experimental import pallas as pl
from jax.experimental.pallas import tpu as pltpu
from jax.sharding import PartitionSpec as P

MESH = pl.DeviceIdType.MESH
CHUNKS = 4


def kernel(nrow, ncol, slab, slab_mask, density, block_mask, out,
           panel, rows, square, cube, up_s, dn_s, y_s, core_s, arrive, arrive_half,
           rows_s, rows_r, sq_s, sq_r):
    height, cols = density.shape
    block = height // block_mask.shape[0]
    half = height // 2
    width = panel.shape[2]
    nchunk = panel.shape[0]
    kblock = rows.shape[2]
    per = cols // kblock
    Z = nrow // 4
    me = lax.axis_index("row")
    mc = lax.axis_index("col")
    z, y, c = me // 4, lax.rem(me // 2, 2), lax.rem(me, 2)
    flip_z = z + 1 - 2 * lax.rem(z, 2)
    flip_y = 1 - y
    up, dn = me + 4, me - 4
    over_y = me + 2 - 4 * y
    over_c = me + 1 - 2 * c
    over_z = me + 4 - 8 * lax.rem(z, 2)

    def row_of(zz, yy, cc):
        return (zz * 2 + yy) * 2 + cc

    for i in range(height // block):
        for k in range(cols // block):
            at_row, at_col = i * block, k * block
            keep = jnp.full((block, block), block_mask[i, k], jnp.int32).astype(jnp.float32).astype(jnp.bfloat16)
            start = pl.multiple_of(me * height + at_row, block)
            panel[at_col // width, pl.ds(start, block), at_col % width:at_col % width + block] = (
                density[at_row:at_row + block, at_col:at_col + block] * keep)
    for i in range(height // block):
        for k in range(cols // block):
            at_row, at_col = i * block, k * block
            keep = jnp.full((block, block), slab_mask[i, k], jnp.int32).astype(jnp.float32).astype(jnp.bfloat16)
            rows[mc * per + at_col // kblock, at_row:at_row + block, at_col % kblock:at_col % kblock + block] = (
                slab[at_row:at_row + block, at_col:at_col + block] * keep)

    barrier = pltpu.get_barrier_semaphore()

    def greet(row):
        pl.semaphore_signal(barrier, inc=1, device_id={"row": row}, device_id_type=MESH)

    pl.when(z < Z - 1)(lambda: greet(up))
    pl.when(z > 0)(lambda: greet(dn))
    greet(over_y)
    greet(over_c)
    for d in range(1, ncol):
        pl.semaphore_signal(barrier, inc=1, device_id={"col": lax.rem(mc + d, ncol)}, device_id_type=MESH)
    pl.semaphore_wait(barrier, (z < Z - 1).astype(jnp.int32) + (z > 0).astype(jnp.int32) + 1 + ncol)

    def copy(j, source, first, count, send, recv, target):
        ref = panel.at[j, pl.ds(pl.multiple_of(source * height + first, half), count), :]
        return pltpu.make_async_remote_copy(
            src_ref=ref, dst_ref=ref, send_sem=send, recv_sem=recv,
            device_id={"row": target}, device_id_type=MESH)

    def full(j, source, send, target):
        return copy(j, source, 0, height, send, arrive.at[j, source], target)

    def top(j, source, send, target):
        return copy(j, source, 0, half, send, arrive.at[j, source], target)

    def to_up(j, zz):
        return full(j, row_of(zz, y, c), up_s.at[j, zz], up)

    def to_dn(j, zz):
        return full(j, row_of(zz, y, c), dn_s.at[j, zz], dn)

    def to_y(j, zz):
        return full(j, row_of(zz, y, c), y_s.at[j, zz], over_y)

    def to_y_top(j, zz):
        return top(j, row_of(zz, y, c), y_s.at[j, zz], over_y)

    def to_core(j, zz, yy):
        return full(j, row_of(zz, yy, c), core_s.at[j, zz * 2 + yy], over_c)

    def to_z_half(j):
        return copy(j, row_of(z, flip_y, c), half, half, up_s.at[j, Z], arrive_half.at[j], over_z)

    def got_full(j, source):
        full(j, source, up_s.at[j, 0], over_c).wait_recv()

    def got_top(j, source):
        top(j, source, up_s.at[j, 0], over_c).wait_recv()

    def got_z_half(j):
        copy(j, row_of(flip_z, flip_y, c), half, half, up_s.at[j, Z], arrive_half.at[j], over_z).wait_recv()

    def send_own(j):
        pl.when(z < Z - 1)(lambda: to_up(j, z).start())
        pl.when(z > 0)(lambda: to_dn(j, z).start())
        to_y(j, z).start()
        to_core(j, z, y).start()

    def pass_y(j, zz, act):
        pl.when(zz == flip_z)(lambda: act(to_y_top(j, zz)))
        pl.when(zz != flip_z)(lambda: act(to_y(j, zz)))

    start = lambda cp: cp.start()
    finish = lambda cp: cp.wait_send()

    def line(j):
        for s in range(1, Z):
            @pl.when(z >= s)
            def _():
                zz = z - s
                got_full(j, row_of(zz, y, c))
                pl.when(z < Z - 1)(lambda: to_up(j, zz).start())
                pass_y(j, zz, start)
                to_core(j, zz, y).start()

            @pl.when(z + s < Z)
            def _():
                zz = z + s
                got_full(j, row_of(zz, y, c))
                pl.when(z > 0)(lambda: to_dn(j, zz).start())
                pass_y(j, zz, start)
                to_core(j, zz, y).start()

            if s == 1:
                got_full(j, row_of(z, flip_y, c))
                to_z_half(j).start()
                to_core(j, z, flip_y).start()

    def others(j):
        got_top(j, row_of(flip_z, flip_y, c))
        got_z_half(j)
        to_core(j, flip_z, flip_y).start()

        def one(zz, _):
            @pl.when((zz != z) & (zz != flip_z))
            def _():
                got_full(j, row_of(zz, flip_y, c))
                to_core(j, zz, flip_y).start()
            return 0
        lax.fori_loop(0, Z, one, 0)

        def two(k, _):
            got_full(j, k * 2 + 1 - c)
            return 0
        lax.fori_loop(0, nrow // 2, two, 0)

    def rows_copy(d):
        ref = rows.at[pl.ds(mc * per, per)]
        return pltpu.make_async_remote_copy(
            src_ref=ref, dst_ref=ref, send_sem=rows_s.at[d], recv_sem=rows_r.at[mc],
            device_id={"col": lax.rem(mc + d, ncol)}, device_id_type=MESH)

    def rows_got(d):
        who = lax.rem(mc + d, ncol)
        ref = rows.at[pl.ds(who * per, per)]
        pltpu.make_async_remote_copy(
            src_ref=ref, dst_ref=ref, send_sem=rows_s.at[d], recv_sem=rows_r.at[who],
            device_id={"col": who}, device_id_type=MESH).wait_recv()

    def sq_copy(j, d):
        ref = square.at[mc * nchunk + j]
        return pltpu.make_async_remote_copy(
            src_ref=ref, dst_ref=ref, send_sem=sq_s.at[j, d], recv_sem=sq_r.at[j, mc],
            device_id={"col": lax.rem(mc + d, ncol)}, device_id_type=MESH)

    def sq_got(j, d):
        who = lax.rem(mc + d, ncol)
        ref = square.at[who * nchunk + j]
        pltpu.make_async_remote_copy(
            src_ref=ref, dst_ref=ref, send_sem=sq_s.at[j, d], recv_sem=sq_r.at[j, who],
            device_id={"col": who}, device_id_type=MESH).wait_recv()

    def make_square(j):
        cube[j] = jnp.zeros(cube.shape[1:], cube.dtype)

        def one(k, _):
            cube[j] += jnp.dot(rows[k], panel[j, pl.ds(pl.multiple_of(k * kblock, kblock), kblock), :],
                               preferred_element_type=jnp.float32)
            return 0
        lax.fori_loop(0, rows.shape[0], one, 0)
        square[mc * nchunk + j] = cube[j].astype(jnp.bfloat16)
        for d in range(1, ncol):
            sq_copy(j, d).start()

    send_own(0)
    for d in range(1, ncol):
        rows_copy(d).start()

    def chunk(t, _):
        pl.when(t + 1 < nchunk)(lambda: send_own(t + 1))
        pl.when(t < nchunk)(lambda: line(t))

        @pl.when(t == 1)
        def _():
            for d in range(1, ncol):
                rows_got(d)

        @pl.when(t >= 1)
        def _():
            others(t - 1)
            make_square(t - 1)
        return 0
    lax.fori_loop(0, nchunk + 1, chunk, 0)

    last = nchunk - 1

    def add(n, at):
        cube[n] += jnp.dot(square[at], panel[n, pl.ds(pl.multiple_of(at * width, width), width), :],
                           preferred_element_type=jnp.float32)

    def clear(n, _):
        cube[n] = jnp.zeros(cube.shape[1:], cube.dtype)
        return 0
    lax.fori_loop(0, nchunk, clear, 0)

    def early(k, _):
        for d in range(1, ncol):
            sq_got(k, d)

        def col(n, _):
            for d in range(ncol):
                add(n, lax.rem(mc + d, ncol) * nchunk + k)
            return 0
        lax.fori_loop(0, nchunk, col, 0)
        return 0
    lax.fori_loop(0, last, early, 0)

    def own(n, _):
        add(n, mc * nchunk + last)
        return 0
    lax.fori_loop(0, nchunk, own, 0)
    for d in range(1, ncol):
        sq_got(last, d)

    def final(n, _):
        for d in range(1, ncol):
            add(n, lax.rem(mc + d, ncol) * nchunk + last)
        out[:, pl.ds(pl.multiple_of(n * width, width), width)] = (
            3.0 * square[mc * nchunk + n].astype(jnp.float32) - 2.0 * cube[n]).astype(out.dtype)
        return 0
    lax.fori_loop(0, nchunk, final, 0)

    def drain(j, _):
        def one(zz, _):
            pl.when((z < Z - 1) & (zz <= z))(lambda: to_up(j, zz).wait_send())
            pl.when((z > 0) & (zz >= z))(lambda: to_dn(j, zz).wait_send())
            pass_y(j, zz, finish)
            to_core(j, zz, y).wait_send()
            to_core(j, zz, flip_y).wait_send()
            return 0
        lax.fori_loop(0, Z, one, 0)
        to_z_half(j).wait_send()
        for d in range(1, ncol):
            sq_copy(j, d).wait_send()
        return 0
    lax.fori_loop(0, nchunk, drain, 0)
    for d in range(1, ncol):
        rows_copy(d).wait_send()


def per_device(nrow, ncol, slab, slab_mask, density, block_mask):
    height, cols = density.shape
    tall = slab.shape[0]
    width = cols // CHUNKS
    zs = nrow // 4
    kblock = cols // 2
    vmem = pl.BlockSpec(memory_space=pltpu.VMEM)
    smem = pl.BlockSpec(memory_space=pltpu.SMEM)
    dma = pltpu.SemaphoreType.DMA
    return pl.pallas_call(
        functools.partial(kernel, nrow, ncol),
        out_shape=jax.ShapeDtypeStruct((tall, cols), jnp.bfloat16),
        in_specs=[vmem, smem, vmem, smem],
        out_specs=vmem,
        scratch_shapes=[
            pltpu.VMEM((CHUNKS, height * nrow, width), jnp.bfloat16),
            pltpu.VMEM((ncol * cols // kblock, tall, kblock), jnp.bfloat16),
            pltpu.VMEM((ncol * CHUNKS, tall, width), jnp.bfloat16),
            pltpu.VMEM((CHUNKS, tall, width), jnp.float32),
            dma((CHUNKS, zs + 1)), dma((CHUNKS, zs)), dma((CHUNKS, zs)), dma((CHUNKS, 2 * zs)),
            dma((CHUNKS, nrow)), dma((CHUNKS,)),
            dma((ncol,)), dma((ncol,)), dma((CHUNKS, ncol)), dma((CHUNKS, ncol)),
        ],
        compiler_params=pltpu.CompilerParams(
            collective_id=0, has_side_effects=True, vmem_limit_bytes=48 * 1024 * 1024),
    )(slab, slab_mask, density, block_mask)


def solution(mesh):
    placed = (P("row", "col"), P("row", "col"), P("row", "col"), P("row", "col"))
    return jax.shard_map(
        functools.partial(per_device, mesh.shape["row"], mesh.shape["col"]),
        mesh=mesh, in_specs=placed, out_specs=P("row", "col"), check_vma=False
    )
```

```python
import functools

import jax
import jax.numpy as jnp
from jax import lax
from jax.experimental import pallas as pl
from jax.experimental.pallas import tpu as pltpu
from jax.sharding import PartitionSpec as P

MESH = pl.DeviceIdType.MESH
CHUNKS = 4


def kernel(nrow, ncol, slab, slab_mask, density, block_mask, out,
           panel, rows, square, cube, up_s, dn_s, y_s, core_s, arrive, arrive_half,
           rows_s, rows_r, sq_s, sq_r):
    height, cols = density.shape
    block = height // block_mask.shape[0]
    half = height // 2
    width = panel.shape[2]
    nchunk = panel.shape[0]
    kblock = rows.shape[2]
    per = cols // kblock
    Z = nrow // 4
    me = lax.axis_index("row")
    mc = lax.axis_index("col")
    z, y, c = me // 4, lax.rem(me // 2, 2), lax.rem(me, 2)
    flip_z = z + 1 - 2 * lax.rem(z, 2)
    flip_y = 1 - y
    up, dn = me + 4, me - 4
    over_y = me + 2 - 4 * y
    over_c = me + 1 - 2 * c
    over_z = me + 4 - 8 * lax.rem(z, 2)

    def row_of(zz, yy, cc):
        return (zz * 2 + yy) * 2 + cc

    for i in range(height // block):
        for k in range(cols // block):
            at_row, at_col = i * block, k * block
            keep = jnp.full((block, block), block_mask[i, k], jnp.int32).astype(jnp.float32).astype(jnp.bfloat16)
            start = pl.multiple_of(me * height + at_row, block)
            panel[at_col // width, pl.ds(start, block), at_col % width:at_col % width + block] = (
                density[at_row:at_row + block, at_col:at_col + block] * keep)
    for i in range(height // block):
        for k in range(cols // block):
            at_row, at_col = i * block, k * block
            keep = jnp.full((block, block), slab_mask[i, k], jnp.int32).astype(jnp.float32).astype(jnp.bfloat16)
            rows[mc * per + at_col // kblock, at_row:at_row + block, at_col % kblock:at_col % kblock + block] = (
                slab[at_row:at_row + block, at_col:at_col + block] * keep)

    barrier = pltpu.get_barrier_semaphore()

    def greet(row):
        pl.semaphore_signal(barrier, inc=1, device_id={"row": row}, device_id_type=MESH)

    pl.when(z < Z - 1)(lambda: greet(up))
    pl.when(z > 0)(lambda: greet(dn))
    greet(over_y)
    greet(over_c)
    for d in range(1, ncol):
        pl.semaphore_signal(barrier, inc=1, device_id={"col": lax.rem(mc + d, ncol)}, device_id_type=MESH)
    pl.semaphore_wait(barrier, (z < Z - 1).astype(jnp.int32) + (z > 0).astype(jnp.int32) + 1 + ncol)

    def copy(j, source, first, count, send, recv, target):
        ref = panel.at[j, pl.ds(pl.multiple_of(source * height + first, half), count), :]
        return pltpu.make_async_remote_copy(
            src_ref=ref, dst_ref=ref, send_sem=send, recv_sem=recv,
            device_id={"row": target}, device_id_type=MESH)

    def full(j, source, send, target):
        return copy(j, source, 0, height, send, arrive.at[j, source], target)

    def top(j, source, send, target):
        return copy(j, source, 0, half, send, arrive.at[j, source], target)

    def to_up(j, zz):
        return full(j, row_of(zz, y, c), up_s.at[j, zz], up)

    def to_dn(j, zz):
        return full(j, row_of(zz, y, c), dn_s.at[j, zz], dn)

    def to_y(j, zz):
        return full(j, row_of(zz, y, c), y_s.at[j, zz], over_y)

    def to_y_top(j, zz):
        return top(j, row_of(zz, y, c), y_s.at[j, zz], over_y)

    def to_core(j, zz, yy):
        return full(j, row_of(zz, yy, c), core_s.at[j, zz * 2 + yy], over_c)

    def to_z_half(j):
        return copy(j, row_of(z, flip_y, c), half, half, up_s.at[j, Z], arrive_half.at[j], over_z)

    def got_full(j, source):
        full(j, source, up_s.at[j, 0], over_c).wait_recv()

    def got_top(j, source):
        top(j, source, up_s.at[j, 0], over_c).wait_recv()

    def got_z_half(j):
        copy(j, row_of(flip_z, flip_y, c), half, half, up_s.at[j, Z], arrive_half.at[j], over_z).wait_recv()

    def send_own(j):
        pl.when(z < Z - 1)(lambda: to_up(j, z).start())
        pl.when(z > 0)(lambda: to_dn(j, z).start())
        to_y(j, z).start()
        to_core(j, z, y).start()

    def pass_y(j, zz, act):
        pl.when(zz == flip_z)(lambda: act(to_y_top(j, zz)))
        pl.when(zz != flip_z)(lambda: act(to_y(j, zz)))

    start = lambda cp: cp.start()
    finish = lambda cp: cp.wait_send()

    def line(j):
        for s in range(1, Z):
            @pl.when(z >= s)
            def _():
                zz = z - s
                got_full(j, row_of(zz, y, c))
                pl.when(z < Z - 1)(lambda: to_up(j, zz).start())
                pass_y(j, zz, start)
                to_core(j, zz, y).start()

            @pl.when(z + s < Z)
            def _():
                zz = z + s
                got_full(j, row_of(zz, y, c))
                pl.when(z > 0)(lambda: to_dn(j, zz).start())
                pass_y(j, zz, start)
                to_core(j, zz, y).start()

            if s == 1:
                got_full(j, row_of(z, flip_y, c))
                to_z_half(j).start()
                to_core(j, z, flip_y).start()

    def others(j):
        got_top(j, row_of(flip_z, flip_y, c))
        got_z_half(j)
        to_core(j, flip_z, flip_y).start()

        def one(zz, _):
            @pl.when((zz != z) & (zz != flip_z))
            def _():
                got_full(j, row_of(zz, flip_y, c))
                to_core(j, zz, flip_y).start()
            return 0
        lax.fori_loop(0, Z, one, 0)

        def two(k, _):
            got_full(j, k * 2 + 1 - c)
            return 0
        lax.fori_loop(0, nrow // 2, two, 0)

    def rows_copy(d):
        ref = rows.at[pl.ds(mc * per, per)]
        return pltpu.make_async_remote_copy(
            src_ref=ref, dst_ref=ref, send_sem=rows_s.at[d], recv_sem=rows_r.at[mc],
            device_id={"col": lax.rem(mc + d, ncol)}, device_id_type=MESH)

    def rows_got(d):
        who = lax.rem(mc + d, ncol)
        ref = rows.at[pl.ds(who * per, per)]
        pltpu.make_async_remote_copy(
            src_ref=ref, dst_ref=ref, send_sem=rows_s.at[d], recv_sem=rows_r.at[who],
            device_id={"col": who}, device_id_type=MESH).wait_recv()

    def sq_copy(j, d):
        ref = square.at[mc * nchunk + j]
        return pltpu.make_async_remote_copy(
            src_ref=ref, dst_ref=ref, send_sem=sq_s.at[j, d], recv_sem=sq_r.at[j, mc],
            device_id={"col": lax.rem(mc + d, ncol)}, device_id_type=MESH)

    def sq_got(j, d):
        who = lax.rem(mc + d, ncol)
        ref = square.at[who * nchunk + j]
        pltpu.make_async_remote_copy(
            src_ref=ref, dst_ref=ref, send_sem=sq_s.at[j, d], recv_sem=sq_r.at[j, who],
            device_id={"col": who}, device_id_type=MESH).wait_recv()

    def make_square(j):
        whole = None
        for k in range(rows.shape[0]):
            part = jnp.dot(rows[k], panel[j, k * kblock:(k + 1) * kblock, :], preferred_element_type=jnp.float32)
            whole = part if whole is None else whole + part
        square[mc * nchunk + j] = whole.astype(jnp.bfloat16)
        for d in range(1, ncol):
            sq_copy(j, d).start()

    send_own(0)
    for d in range(1, ncol):
        rows_copy(d).start()

    def chunk(t, _):
        pl.when(t + 1 < nchunk)(lambda: send_own(t + 1))
        pl.when(t < nchunk)(lambda: line(t))

        @pl.when(t == 1)
        def _():
            for d in range(1, ncol):
                rows_got(d)

        @pl.when(t >= 1)
        def _():
            others(t - 1)
            make_square(t - 1)
        return 0
    lax.fori_loop(0, nchunk + 1, chunk, 0)

    last = nchunk - 1

    def term(n, at):
        return jnp.dot(square[at], panel[n, pl.ds(pl.multiple_of(at * width, width), width), :],
                       preferred_element_type=jnp.float32)

    for k in range(last):
        for d in range(1, ncol):
            sq_got(k, d)

    def early(n, _):
        whole = term(n, mc * nchunk + last)
        for k in range(last):
            for d in range(ncol):
                whole = whole + term(n, lax.rem(mc + d, ncol) * nchunk + k)
        cube[n] = whole
        return 0
    lax.fori_loop(0, nchunk, early, 0)
    for d in range(1, ncol):
        sq_got(last, d)

    def final(n, _):
        whole = cube[n]
        for d in range(1, ncol):
            whole = whole + term(n, lax.rem(mc + d, ncol) * nchunk + last)
        out[:, pl.ds(pl.multiple_of(n * width, width), width)] = (
            3.0 * square[mc * nchunk + n].astype(jnp.float32) - 2.0 * whole).astype(out.dtype)
        return 0
    lax.fori_loop(0, nchunk, final, 0)

    def drain(j, _):
        def one(zz, _):
            pl.when((z < Z - 1) & (zz <= z))(lambda: to_up(j, zz).wait_send())
            pl.when((z > 0) & (zz >= z))(lambda: to_dn(j, zz).wait_send())
            pass_y(j, zz, finish)
            to_core(j, zz, y).wait_send()
            to_core(j, zz, flip_y).wait_send()
            return 0
        lax.fori_loop(0, Z, one, 0)
        to_z_half(j).wait_send()
        for d in range(1, ncol):
            sq_copy(j, d).wait_send()
        return 0
    lax.fori_loop(0, nchunk, drain, 0)
    for d in range(1, ncol):
        rows_copy(d).wait_send()


def per_device(nrow, ncol, slab, slab_mask, density, block_mask):
    height, cols = density.shape
    tall = slab.shape[0]
    width = cols // CHUNKS
    zs = nrow // 4
    kblock = cols // 2
    vmem = pl.BlockSpec(memory_space=pltpu.VMEM)
    smem = pl.BlockSpec(memory_space=pltpu.SMEM)
    dma = pltpu.SemaphoreType.DMA
    return pl.pallas_call(
        functools.partial(kernel, nrow, ncol),
        out_shape=jax.ShapeDtypeStruct((tall, cols), jnp.bfloat16),
        in_specs=[vmem, smem, vmem, smem],
        out_specs=vmem,
        scratch_shapes=[
            pltpu.VMEM((CHUNKS, height * nrow, width), jnp.bfloat16),
            pltpu.VMEM((ncol * cols // kblock, tall, kblock), jnp.bfloat16),
            pltpu.VMEM((ncol * CHUNKS, tall, width), jnp.bfloat16),
            pltpu.VMEM((CHUNKS, tall, width), jnp.float32),
            dma((CHUNKS, zs + 1)), dma((CHUNKS, zs)), dma((CHUNKS, zs)), dma((CHUNKS, 2 * zs)),
            dma((CHUNKS, nrow)), dma((CHUNKS,)),
            dma((ncol,)), dma((ncol,)), dma((CHUNKS, ncol)), dma((CHUNKS, ncol)),
        ],
        compiler_params=pltpu.CompilerParams(
            collective_id=0, has_side_effects=True, vmem_limit_bytes=48 * 1024 * 1024),
    )(slab, slab_mask, density, block_mask)


def solution(mesh):
    placed = (P("row", "col"), P("row", "col"), P("row", "col"), P("row", "col"))
    return jax.shard_map(
        functools.partial(per_device, mesh.shape["row"], mesh.shape["col"]),
        mesh=mesh, in_specs=placed, out_specs=P("row", "col"), check_vma=False
    )
```
